32 devices in a mesh: row: 8 (over y, x, core), col: 4 (over z).
Axes of the slice: x: 2, y: 2, z: 4, core: 2. Of those that a mesh axis runs over, the one named last changes fastest.
Arguments:
- gradient: bfloat16 [24576, 24576], P('row', 'col'), may hold values from -6 to 6
- sensitivity: bfloat16 [24576, 16384], P('row', 'col'), may hold values from -0.0390625 to 0.0390625
Outputs:
- influence: float32 [512, 16384], P('row', 'col')
The draws below stay inside these ranges and needn't reach their ends.
All inputs are finite; a program needn't handle non-finite values.
Results may differ from the reference program's by a relative error of at most 0.0029.
Values may be sent and summed in bfloat16 or wider, within the bound.
A program may use at most 128 MiB of HBM per device.

```python
import jax
import jax.numpy as jnp
from jax import lax

N = 24576
M = 16384
PANEL = 512


def block_levels(own_key, extent, shards, smallest, largest):
    gain, own = 1.0, jax.random.fold_in(own_key, 6)
    for position, parts in shards:
        heights = jnp.exp(jax.random.uniform(jax.random.fold_in(own, position), (parts,), jnp.float32, smallest / len(shards), largest / len(shards)))
        gain = gain * jnp.repeat(heights, extent[position] // parts).reshape([-1 if axis == position else 1 for axis in range(len(extent))])
    return gain


def noise(own_key, dims, spread, limit, cuts=(), held_as=jnp.bfloat16):
    loudness = block_levels(own_key, dims, cuts, -0.22, 0.18) if cuts else 1.0
    values = jax.random.normal(own_key, dims, jnp.float32) * spread * loudness
    return jnp.minimum(jnp.maximum(values, -limit), limit).astype(held_as)


def setup_inputs(seed: int = 0) -> dict:
    seeds = jax.random.split(jax.random.key(seed), 3)
    gradient = noise(seeds[0], (N, N), 1.0, 6.0, ((0, 8), (1, 4)))
    sensitivity = noise(seeds[1], (N, M), N ** -0.5, 0.0390625, ((0, 8), (1, 4)))
    return {"gradient": gradient, "sensitivity": sensitivity}


def reference(gradient, sensitivity):
    panel = sensitivity[:, :PANEL]
    image = jnp.dot(gradient, panel, preferred_element_type=jnp.float32).astype(jnp.bfloat16)
    return lax.dot_general(image, sensitivity, (((0,), (0,)), ((), ())), preferred_element_type=jnp.float32)
```

```python
import functools

import jax
import jax.numpy as jnp
from jax import lax
from jax.experimental import pallas as pl
from jax.experimental.pallas import tpu as pltpu
from jax.sharding import PartitionSpec as P

PANEL = 512
TM = 256
TK = 768
TN = 512
MESH = pl.DeviceIdType.MESH


def kernel(R, C, grad, sens, out, panel, ybuf, own, rbuf, image, acc, sbuf, obuf, gbuf, vbuf, yacc, image_t,
           gsem, vsem, lsem, sc_s, sc_r, pg_s, pg_r, sb_s, sb_r, y_s, y_r, ag_s, ag_r, ps_s, ps_r, os_s, os_r):
    r, c = lax.axis_index("row"), lax.axis_index("col")
    ratio = R // C
    chips = R // 2
    core = lax.rem(r, 2)
    chip = r // 2
    sib = r + 1 - 2 * core
    rows, kdim = grad.shape
    width = sens.shape[1]
    T = rows // TM
    q = TM // C
    piece = kdim // R
    nsub = sc_r.shape[0]
    sub = piece // nsub
    po = PANEL // R

    def remote(src, dst, ssem, rsem, row, col):
        return pltpu.make_async_remote_copy(src_ref=src, dst_ref=dst, send_sem=ssem, recv_sem=rsem,
                                            device_id=(row, col), device_id_type=MESH)

    def load_g(t, slot):
        return pltpu.make_async_copy(grad.at[pl.ds(pl.multiple_of(t * TM, TM), TM)], gbuf.at[slot], gsem.at[slot])

    def load_v(t, slot):
        return pltpu.make_async_copy(sens.at[pl.ds(pl.multiple_of(t * TM, TM), TM)], vbuf.at[slot], vsem.at[slot])

    for t in range(min(2, T)):
        load_g(t, t).start()
        load_v(t, t).start()

    src_row = c * ratio + r // C
    self_fed = jnp.logical_and(c == 0, src_row == r)
    bar = pltpu.get_barrier_semaphore()
    for d in range(1, R):
        pl.semaphore_signal(bar, inc=1, device_id=(lax.rem(r + d, R), c), device_id_type=MESH)
    for d in range(1, C):
        pl.semaphore_signal(bar, inc=1, device_id=(r, lax.rem(c + d, C)), device_id_type=MESH)

    @pl.when(jnp.logical_not(self_fed))
    def _():
        pl.semaphore_signal(bar, inc=1, device_id=(src_row, 0), device_id_type=MESH)

    fed = jnp.where(c == 0, C, 0) - jnp.where(self_fed, 1, 0)
    pl.semaphore_wait(bar, R - 1 + C - 1 + fed)

    def prow(k, s):
        return panel.at[pl.ds(pl.multiple_of(k * piece + s * sub, sub), sub)]

    def scatter(j, s):
        k = lax.rem(r, ratio) * C + j
        src = sens.at[pl.ds(j * piece + s * sub, sub), pl.ds(0, PANEL)]
        return k, src, remote(src, prow(k, s), sc_s.at[j * nsub + s], sc_r.at[s], k, r // ratio)

    def is_self(j):
        return jnp.logical_and(r // ratio == 0, lax.rem(r, ratio) * C + j == r)

    def local(j, s):
        k, src, _ = scatter(j, s)
        return pltpu.make_async_copy(src, prow(k, s), lsem.at[s])

    @pl.when(c == 0)
    def _():
        for s in range(nsub):
            for j in range(C):
                @pl.when(is_self(j))
                def _():
                    local(j, s).start()

                @pl.when(jnp.logical_not(is_self(j)))
                def _():
                    scatter(j, s)[2].start()

    def gather(d, s):
        to = lax.rem(chip + d, chips) * 2 + core
        return remote(prow(r, s), prow(r, s), pg_s.at[(d - 1) * nsub + s], pg_r.at[(d - 1) * nsub + s], to, c)

    def to_sib(d, s):
        k = lax.rem(chip + chips - d, chips) * 2 + core
        return remote(prow(k, s), prow(k, s), sb_s.at[d * nsub + s], sb_r.at[d * nsub + s], sib, c)

    for s in range(nsub):
        @pl.when(self_fed)
        def _():
            local(0, s).wait()

        @pl.when(jnp.logical_not(self_fed))
        def _():
            remote(prow(r, s), prow(r, s), sc_s.at[s], sc_r.at[s], sib, c).wait_recv()

        for d in range(1, chips):
            gather(d, s).start()
        to_sib(0, s).start()
    for s in range(nsub):
        for d in range(1, chips):
            gather(d, s).wait_recv()
            to_sib(d, s).start()
    for s in range(nsub):
        for d in range(chips):
            to_sib(d, s).wait_recv()

    def y_copy(t, d):
        to = lax.rem(c + d, C)
        i = t * (C - 1) + d - 1
        return remote(ybuf.at[t, pl.ds(pl.multiple_of(to * q, q), q)], rbuf.at[i], y_s.at[i], y_r.at[i], r, to)

    def first(t, carry):
        slot = lax.rem(t, 2)
        load_g(t, slot).wait()
        yacc[...] = jnp.zeros_like(yacc)

        def step(k, carry):
            at = pl.ds(pl.multiple_of(k * TK, TK), TK)
            yacc[...] += jnp.dot(gbuf[slot, :, at], panel[at, :], preferred_element_type=jnp.float32)
            return carry

        lax.fori_loop(0, kdim // TK, step, 0)

        @pl.when(t + 2 < T)
        def _():
            load_g(t + 2, slot).start()

        ybuf[t] = yacc[...].astype(jnp.bfloat16)
        own[t] = yacc[pl.ds(pl.multiple_of(c * q, q), q), :]
        for d in range(1, C):
            y_copy(t, d).start()
        return carry

    lax.fori_loop(0, T, first, 0)
    acc[...] = jnp.zeros_like(acc)

    def ag(t, s, way):
        owner, to = (c - s, c + 1) if way == 0 else (c + s, c - 1)
        i = (t * (C - 1) + s) * 2 + way
        block = image.at[t, pl.ds(pl.multiple_of(owner * q, q), q)]
        return remote(block, block, ag_s.at[i], ag_r.at[i], r, to)

    def ag_cond(s, way):
        if way == 0:
            return jnp.logical_and(c - s >= 0, c + 1 < C)
        return jnp.logical_and(c + s < C, c - 1 >= 0)

    def ag_recv(t, s, way):
        owner = c - s if way == 0 else c + s
        i = (t * (C - 1) + s - 1) * 2 + way
        block = image.at[t, pl.ds(pl.multiple_of(owner * q, q), q)]
        return remote(block, block, ag_s.at[i], ag_r.at[i], r, lax.rem(c + 1, C))

    def send_on(t, s):
        for way in range(2):
            @pl.when(ag_cond(s, way))
            def _():
                ag(t, s, way).start()

    def second(u, carry):
        @pl.when(u < T)
        def _():
            total = own[u]
            for d in range(1, C):
                y_copy(u, d).wait_recv()
                total = total + rbuf[u * (C - 1) + d - 1].astype(jnp.float32)
            image[u, pl.ds(pl.multiple_of(c * q, q), q)] = total.astype(jnp.bfloat16)
            send_on(u, 0)

        for s in range(1, C):
            t = u - s

            @pl.when(jnp.logical_and(t >= 0, t < T))
            def _():
                @pl.when(c - s >= 0)
                def _():
                    ag_recv(t, s, 0).wait_recv()

                @pl.when(c + s < C)
                def _():
                    ag_recv(t, s, 1).wait_recv()

                if s < C - 1:
                    send_on(t, s)

        @pl.when(u >= C - 1)
        def _():
            t = u - (C - 1)
            slot = lax.rem(t, 2)
            load_v(t, slot).wait()
            image_t[...] = image[t].T

            def step(n, carry):
                at = pl.ds(pl.multiple_of(n * TN, TN), TN)
                acc[:, at] += jnp.dot(image_t[...], vbuf[slot, :, at], preferred_element_type=jnp.float32)
                return carry

            lax.fori_loop(0, width // TN, step, 0)

            @pl.when(t + 2 < T)
            def _():
                load_v(t + 2, slot).start()

        return carry

    lax.fori_loop(0, T + C - 1, second, 0)

    def arow(k):
        return acc.at[pl.ds(pl.multiple_of(k * po, po), po)]

    def pair(d):
        to = lax.rem(chip + d, chips)
        return remote(arow(to * 2 + 1 - core), sbuf.at[d], ps_s.at[d], ps_r.at[d], sib, c)

    def spread(d):
        k = lax.rem(chip + d, chips) * 2 + core
        return remote(arow(k), obuf.at[d - 1], os_s.at[d - 1], os_r.at[d - 1], k, c)

    order = list(range(1, chips)) + [0]
    for d in order:
        pair(d).start()
    for d in order:
        pair(d).wait_recv()
        k = lax.rem(chip + d, chips) * 2 + core
        at = pl.ds(pl.multiple_of(k * po, po), po)
        acc[at, :] += sbuf[d]
        if d:
            spread(d).start()
    mine = pl.ds(pl.multiple_of(r * po, po), po)
    for d in range(1, chips):
        spread(d).wait_recv()
        acc[mine, :] += obuf[d - 1]
    out[...] = acc[mine, :]

    @pl.when(c == 0)
    def _():
        for s in range(nsub):
            for j in range(C):
                @pl.when(jnp.logical_not(is_self(j)))
                def _():
                    scatter(j, s)[2].wait_send()

    for s in range(nsub):
        for d in range(1, chips):
            gather(d, s).wait_send()
        for d in range(chips):
            to_sib(d, s).wait_send()

    def drain(t, carry):
        for d in range(1, C):
            y_copy(t, d).wait_send()
        for s in range(C - 1):
            for way in range(2):
                @pl.when(ag_cond(s, way))
                def _():
                    ag(t, s, way).wait_send()
        return carry

    lax.fori_loop(0, T, drain, 0)
    for d in range(chips):
        pair(d).wait_send()
    for d in range(1, chips):
        spread(d).wait_send()


def shards(R, C, gradient, sensitivity):
    rows, kdim = gradient.shape
    width = sensitivity.shape[1]
    T, q, piece, po, chips = rows // TM, TM // C, kdim // R, PANEL // R, R // 2
    nsub = 4 if piece % 64 == 0 else 1
    dma = lambda n: pltpu.SemaphoreType.DMA((n,))
    return pl.pallas_call(
        functools.partial(kernel, R, C),
        out_shape=jax.ShapeDtypeStruct((po, width), jnp.float32),
        in_specs=[pl.BlockSpec(memory_space=pl.ANY)] * 2,
        out_specs=pl.BlockSpec(memory_space=pltpu.VMEM),
        scratch_shapes=[
            pltpu.VMEM((kdim, PANEL), jnp.bfloat16),
            pltpu.VMEM((T, TM, PANEL), jnp.bfloat16),
            pltpu.VMEM((T, q, PANEL), jnp.float32),
            pltpu.VMEM((T * (C - 1), q, PANEL), jnp.bfloat16),
            pltpu.VMEM((T, TM, PANEL), jnp.bfloat16),
            pltpu.VMEM((PANEL, width), jnp.float32),
            pltpu.VMEM((chips, po, width), jnp.float32),
            pltpu.VMEM((chips - 1, po, width), jnp.float32),
            pltpu.VMEM((2, TM, kdim), jnp.bfloat16),
            pltpu.VMEM((2, TM, width), jnp.bfloat16),
            pltpu.VMEM((TM, PANEL), jnp.float32),
            pltpu.VMEM((PANEL, TM), jnp.bfloat16),
            dma(2), dma(2), dma(nsub),
            dma(C * nsub), dma(nsub),
            dma((chips - 1) * nsub), dma((chips - 1) * nsub),
            dma(chips * nsub), dma(chips * nsub),
            dma(T * (C - 1)), dma(T * (C - 1)),
            dma(T * (C - 1) * 2), dma(T * (C - 1) * 2),
            dma(chips), dma(chips),
            dma(chips - 1), dma(chips - 1),
        ],
        compiler_params=pltpu.CompilerParams(
            collective_id=0, has_side_effects=True, vmem_limit_bytes=58 * 2**20
        ),
    )(gradient, sensitivity)


def solution(mesh):
    R, C = mesh.shape["row"], mesh.shape["col"]
    return jax.shard_map(
        functools.partial(shards, R, C),
        mesh=mesh,
        in_specs=(P("row", "col"), P("row", "col")),
        out_specs=P("row", "col"),
        check_vma=False,
    )
```

```python
import functools

import jax
import jax.numpy as jnp
from jax import lax
from jax.experimental import pallas as pl
from jax.experimental.pallas import tpu as pltpu
from jax.sharding import PartitionSpec as P

PANEL = 512
HALF = PANEL // 2
TK = 768
TN = 512
MESH = pl.DeviceIdType.MESH


def kernel(R, C, TM, grad, sens, source, out, panel, ybuf, own, rbuf, image, acc, sbuf, obuf, gbuf, vbuf, yacc, image_t,
           gsem, vsem, lsem, sc_s, sc_r, pg_s, pg_r, sb_s, sb_r, y_s, y_r, ag_s, ag_r, ps_s, ps_r, os_s, os_r):
    r, c = lax.axis_index("row"), lax.axis_index("col")
    ratio = R // C
    chips = R // 2
    core = lax.rem(r, 2)
    chip = r // 2
    sib = r + 1 - 2 * core
    rows, kdim = grad.shape
    width = sens.shape[1]
    T = rows // TM
    q = TM // C
    piece = kdim // R
    nsub = sc_r.shape[0] // 2
    sub = piece // nsub
    hp = PANEL // R // 2

    def remote(src, dst, ssem, rsem, row, col):
        return pltpu.make_async_remote_copy(src_ref=src, dst_ref=dst, send_sem=ssem, recv_sem=rsem,
                                            device_id=(row, col), device_id_type=MESH)

    def load(ref, buf, sem, tt):
        at = pl.ds(pl.multiple_of(lax.rem(tt, T) * TM, TM), TM)
        slot = lax.rem(tt, 2)
        return pltpu.make_async_copy(ref.at[at], buf.at[slot], sem.at[slot])

    def load_g(tt):
        return load(grad, gbuf, gsem, tt)

    def load_v(tt):
        return load(sens, vbuf, vsem, tt)

    for t in range(2):
        load_g(t).start()
        load_v(t).start()

    src_row = c * ratio + r // C
    self_fed = jnp.logical_and(c == 0, src_row == r)
    bar = pltpu.get_barrier_semaphore()
    for d in range(1, R):
        pl.semaphore_signal(bar, inc=1, device_id=(lax.rem(r + d, R), c), device_id_type=MESH)
    for d in range(1, C):
        pl.semaphore_signal(bar, inc=1, device_id=(r, lax.rem(c + d, C)), device_id_type=MESH)

    @pl.when(jnp.logical_not(self_fed))
    def _():
        pl.semaphore_signal(bar, inc=1, device_id=(src_row, 0), device_id_type=MESH)

    fed = jnp.where(c == 0, C, 0) - jnp.where(self_fed, 1, 0)
    pl.semaphore_wait(bar, R - 1 + C - 1 + fed)

    def prow(h, k, s):
        return panel.at[h, pl.ds(pl.multiple_of(k * piece + s * sub, sub), sub)]

    def source_at(h, j, s):
        return source.at[pl.ds(j * piece + s * sub, sub), pl.ds(h * HALF, HALF)]

    def scatter(h, j, s):
        k = lax.rem(r, ratio) * C + j
        i = h * nsub + s
        return remote(source_at(h, j, s), prow(h, k, s), sc_s.at[i * C + j], sc_r.at[i], k, r // ratio)

    def is_self(j):
        return jnp.logical_and(r // ratio == 0, lax.rem(r, ratio) * C + j == r)

    def local(h, j, s):
        k = lax.rem(r, ratio) * C + j
        return pltpu.make_async_copy(source_at(h, j, s), prow(h, k, s), lsem.at[h * nsub + s])

    @pl.when(c == 0)
    def _():
        for h in range(2):
            for s in range(nsub):
                for j in range(C):
                    @pl.when(is_self(j))
                    def _():
                        local(h, j, s).start()

                    @pl.when(jnp.logical_not(is_self(j)))
                    def _():
                        scatter(h, j, s).start()

    def gather(h, d, s):
        to = lax.rem(chip + d, chips) * 2 + core
        i = ((d - 1) * 2 + h) * nsub + s
        return remote(prow(h, r, s), prow(h, r, s), pg_s.at[i], pg_r.at[i], to, c)

    def to_sib(h, d, s):
        k = lax.rem(chip + chips - d, chips) * 2 + core
        i = (d * 2 + h) * nsub + s
        return remote(prow(h, k, s), prow(h, k, s), sb_s.at[i], sb_r.at[i], sib, c)

    def relay(h, s):
        @pl.when(self_fed)
        def _():
            local(h, 0, s).wait()

        @pl.when(jnp.logical_not(self_fed))
        def _():
            i = h * nsub + s
            remote(prow(h, r, s), prow(h, r, s), sc_s.at[i], sc_r.at[i], sib, c).wait_recv()

        for d in range(1, chips):
            gather(h, d, s).start()
        to_sib(h, 0, s).start()

    def relay_in(h, s):
        for d in range(1, chips):
            gather(h, d, s).wait_recv()
            to_sib(h, d, s).start()

    def complete(h):
        for s in range(nsub):
            for d in range(chips):
                to_sib(h, d, s).wait_recv()

    def y_copy(t, d):
        to = lax.rem(c + d, C)
        i = t * (C - 1) + d - 1
        return remote(ybuf.at[t, pl.ds(pl.multiple_of(to * q, q), q)], rbuf.at[i], y_s.at[i], y_r.at[i], r, to)

    def first(h, t, carry):
        tt = h * T + t
        slot = lax.rem(tt, 2)
        load_g(tt).wait()
        yacc[...] = jnp.zeros_like(yacc)

        def step(k, carry):
            at = pl.ds(pl.multiple_of(k * TK, TK), TK)
            yacc[...] += jnp.dot(gbuf[slot, :, at], panel[h, at, :], preferred_element_type=jnp.float32)
            return carry

        lax.fori_loop(0, kdim // TK, step, 0)

        @pl.when(tt + 2 < 2 * T)
        def _():
            load_g(tt + 2).start()

        ybuf[tt] = yacc[...].astype(jnp.bfloat16)
        own[tt] = yacc[pl.ds(pl.multiple_of(c * q, q), q), :]
        for d in range(1, C):
            y_copy(tt, d).start()
        return carry

    def ag(t, s, way):
        owner, to = (c - s, c + 1) if way == 0 else (c + s, c - 1)
        i = (t * (C - 1) + s) * 2 + way
        block = image.at[t, pl.ds(pl.multiple_of(owner * q, q), q)]
        return remote(block, block, ag_s.at[i], ag_r.at[i], r, to)

    def ag_cond(s, way):
        if way == 0:
            return jnp.logical_and(c - s >= 0, c + 1 < C)
        return jnp.logical_and(c + s < C, c - 1 >= 0)

    def ag_recv(t, s, way):
        owner = c - s if way == 0 else c + s
        i = (t * (C - 1) + s - 1) * 2 + way
        block = image.at[t, pl.ds(pl.multiple_of(owner * q, q), q)]
        return remote(block, block, ag_s.at[i], ag_r.at[i], r, lax.rem(c + 1, C))

    def send_on(t, s):
        for way in range(2):
            @pl.when(ag_cond(s, way))
            def _():
                ag(t, s, way).start()

    def second(h, u, carry):
        @pl.when(u < T)
        def _():
            tt = h * T + u
            total = own[tt]
            for d in range(1, C):
                y_copy(tt, d).wait_recv()
                total = total + rbuf[tt * (C - 1) + d - 1].astype(jnp.float32)
            image[tt, pl.ds(pl.multiple_of(c * q, q), q)] = total.astype(jnp.bfloat16)
            send_on(tt, 0)

        for s in range(1, C):
            t = u - s

            @pl.when(jnp.logical_and(t >= 0, t < T))
            def _():
                tt = h * T + t

                @pl.when(c - s >= 0)
                def _():
                    ag_recv(tt, s, 0).wait_recv()

                @pl.when(c + s < C)
                def _():
                    ag_recv(tt, s, 1).wait_recv()

                if s < C - 1:
                    send_on(tt, s)

        @pl.when(u >= C - 1)
        def _():
            tt = h * T + u - (C - 1)
            slot = lax.rem(tt, 2)
            load_v(tt).wait()
            image_t[...] = image[tt].T

            def step(n, carry):
                at = pl.ds(pl.multiple_of(n * TN, TN), TN)
                acc[h, :, at] += jnp.dot(image_t[...], vbuf[slot, :, at], preferred_element_type=jnp.float32)
                return carry

            lax.fori_loop(0, width // TN, step, 0)

            @pl.when(tt + 2 < 2 * T)
            def _():
                load_v(tt + 2).start()

        return carry

    def arow(h, k):
        return acc.at[h, pl.ds(pl.multiple_of(k * hp, hp), hp)]

    def pair(h, d):
        to = lax.rem(chip + d, chips)
        i = h * chips + d
        return remote(arow(h, to * 2 + 1 - core), sbuf.at[i], ps_s.at[i], ps_r.at[i], sib, c)

    def spread(h, d):
        k = lax.rem(chip + d, chips) * 2 + core
        i = h * (chips - 1) + d - 1
        return remote(arow(h, k), obuf.at[i], os_s.at[i], os_r.at[i], k, c)

    order = list(range(1, chips)) + [0]

    def out_pair(h):
        for d in order:
            pair(h, d).start()

    def out_spread(h):
        for d in order:
            pair(h, d).wait_recv()
            k = lax.rem(chip + d, chips) * 2 + core
            at = pl.ds(pl.multiple_of(k * hp, hp), hp)
            acc[h, at, :] += sbuf[h * chips + d]
            if d:
                spread(h, d).start()

    def out_sum(h):
        total = acc[h, pl.ds(pl.multiple_of(r * hp, hp), hp), :]
        for d in range(1, chips):
            spread(h, d).wait_recv()
            total = total + obuf[h * (chips - 1) + d - 1]
        out[pl.ds(h * hp, hp), :] = total

    for s in range(nsub):
        relay(0, s)
    for s in range(nsub):
        relay_in(0, s)
    complete(0)
    for s in range(nsub):
        relay(1, s)
        lax.fori_loop(T * s // nsub, T * (s + 1) // nsub, functools.partial(first, 0), 0)
        if s:
            relay_in(1, s - 1)
    relay_in(1, nsub - 1)
    complete(1)
    lax.fori_loop(0, T, functools.partial(first, 1), 0)
    acc[...] = jnp.zeros_like(acc)
    steps = T + C - 1
    lax.fori_loop(0, steps, functools.partial(second, 0), 0)
    out_pair(0)
    lax.fori_loop(0, 1, functools.partial(second, 1), 0)
    out_spread(0)
    lax.fori_loop(1, steps, functools.partial(second, 1), 0)
    out_pair(1)
    out_sum(0)
    out_spread(1)
    out_sum(1)

    for h in range(2):
        @pl.when(c == 0)
        def _():
            for s in range(nsub):
                for j in range(C):
                    @pl.when(jnp.logical_not(is_self(j)))
                    def _():
                        scatter(h, j, s).wait_send()

        for s in range(nsub):
            for d in range(1, chips):
                gather(h, d, s).wait_send()
            for d in range(chips):
                to_sib(h, d, s).wait_send()

    def drain(t, carry):
        for d in range(1, C):
            y_copy(t, d).wait_send()
        for s in range(C - 1):
            for way in range(2):
                @pl.when(ag_cond(s, way))
                def _():
                    ag(t, s, way).wait_send()
        return carry

    lax.fori_loop(0, 2 * T, drain, 0)
    for h in range(2):
        for d in range(chips):
            pair(h, d).wait_send()
        for d in range(1, chips):
            spread(h, d).wait_send()


def shards(R, C, gradient, sensitivity):
    rows, kdim = gradient.shape
    width = sensitivity.shape[1]
    TM = 512 if rows % 512 == 0 else 256
    T, q, piece, po, chips = rows // TM, TM // C, kdim // R, PANEL // R, R // 2
    hp = po // 2
    nsub = 4 if piece % 64 == 0 else 1
    n = jnp.arange(PANEL)
    h, k, i = n // HALF, n % HALF // hp, n % hp
    taken = k * po + h * hp + i
    pick = (jnp.arange(PANEL)[:, None] == taken[None, :]).astype(jnp.bfloat16)
    source = jnp.dot(sensitivity[:, :PANEL], pick, preferred_element_type=jnp.bfloat16)
    dma = lambda n: pltpu.SemaphoreType.DMA((n,))
    return pl.pallas_call(
        functools.partial(kernel, R, C, TM),
        out_shape=jax.ShapeDtypeStruct((po, width), jnp.float32),
        in_specs=[pl.BlockSpec(memory_space=pl.ANY)] * 3,
        out_specs=pl.BlockSpec(memory_space=pltpu.VMEM),
        scratch_shapes=[
            pltpu.VMEM((2, kdim, HALF), jnp.bfloat16),
            pltpu.VMEM((2 * T, TM, HALF), jnp.bfloat16),
            pltpu.VMEM((2 * T, q, HALF), jnp.float32),
            pltpu.VMEM((2 * T * (C - 1), q, HALF), jnp.bfloat16),
            pltpu.VMEM((2 * T, TM, HALF), jnp.bfloat16),
            pltpu.VMEM((2, HALF, width), jnp.float32),
            pltpu.VMEM((2 * chips, hp, width), jnp.float32),
            pltpu.VMEM((2 * (chips - 1), hp, width), jnp.float32),
            pltpu.VMEM((2, TM, kdim), jnp.bfloat16),
            pltpu.VMEM((2, TM, width), jnp.bfloat16),
            pltpu.VMEM((TM, HALF), jnp.float32),
            pltpu.VMEM((HALF, TM), jnp.bfloat16),
            dma(2), dma(2), dma(2 * nsub),
            dma(2 * C * nsub), dma(2 * nsub),
            dma(2 * (chips - 1) * nsub), dma(2 * (chips - 1) * nsub),
            dma(2 * chips * nsub), dma(2 * chips * nsub),
            dma(2 * T * (C - 1)), dma(2 * T * (C - 1)),
            dma(4 * T * (C - 1)), dma(4 * T * (C - 1)),
            dma(2 * chips), dma(2 * chips),
            dma(2 * (chips - 1)), dma(2 * (chips - 1)),
        ],
        compiler_params=pltpu.CompilerParams(
            collective_id=0, has_side_effects=True, vmem_limit_bytes=60 * 2**20
        ),
    )(gradient, sensitivity, source)


def solution(mesh):
    R, C = mesh.shape["row"], mesh.shape["col"]
    return jax.shard_map(
        functools.partial(shards, R, C),
        mesh=mesh,
        in_specs=(P("row", "col"), P("row", "col")),
        out_specs=P("row", "col"),
        check_vma=False,
    )
```

```python
import functools

import jax
import jax.numpy as jnp
from jax import lax
from jax.experimental import pallas as pl
from jax.experimental.pallas import tpu as pltpu
from jax.sharding import PartitionSpec as P

PANEL = 512
HALF = PANEL // 2
TK = 768
TN = 512
MESH = pl.DeviceIdType.MESH


def kernel(R, C, TM, grad, sens, source, out, panel, ybuf, own, rbuf, image, acc, sbuf, obuf, gbuf, vbuf, yacc, image_t,
           gsem, vsem, lsem, sc_s, sc_r, pg_s, pg_r, sb_s, sb_r, y_s, y_r, ag_s, ag_r, ps_s, ps_r, os_s, os_r):
    r, c = lax.axis_index("row"), lax.axis_index("col")
    ratio = R // C
    chips = R // 2
    core = lax.rem(r, 2)
    chip = r // 2
    sib = r + 1 - 2 * core
    rows, kdim = grad.shape
    width = sens.shape[1]
    T = rows // TM
    q = TM // C
    piece = kdim // R
    nsub = sc_r.shape[0] // 2
    sub = piece // nsub
    hp = PANEL // R // 2

    def remote(src, dst, ssem, rsem, row, col):
        return pltpu.make_async_remote_copy(src_ref=src, dst_ref=dst, send_sem=ssem, recv_sem=rsem,
                                            device_id=(row, col), device_id_type=MESH)

    def load(ref, buf, sem, tt):
        at = pl.ds(pl.multiple_of(lax.rem(tt, T) * TM, TM), TM)
        slot = lax.rem(tt, 2)
        return pltpu.make_async_copy(ref.at[at], buf.at[slot], sem.at[slot])

    def load_g(tt):
        return load(grad, gbuf, gsem, tt)

    def load_v(tt):
        return load(sens, vbuf, vsem, tt)

    for t in range(2):
        load_g(t).start()
        load_v(t).start()

    src_row = c * ratio + r // C
    self_fed = jnp.logical_and(c == 0, src_row == r)
    bar = pltpu.get_barrier_semaphore()
    for d in range(1, R):
        pl.semaphore_signal(bar, inc=1, device_id=(lax.rem(r + d, R), c), device_id_type=MESH)
    for d in range(1, C):
        pl.semaphore_signal(bar, inc=1, device_id=(r, lax.rem(c + d, C)), device_id_type=MESH)

    @pl.when(jnp.logical_not(self_fed))
    def _():
        pl.semaphore_signal(bar, inc=1, device_id=(src_row, 0), device_id_type=MESH)

    fed = jnp.where(c == 0, C, 0) - jnp.where(self_fed, 1, 0)
    pl.semaphore_wait(bar, R - 1 + C - 1 + fed)

    def prow(h, k, s):
        return panel.at[h, pl.ds(pl.multiple_of(k * piece + s * sub, sub), sub)]

    def source_at(h, j, s):
        return source.at[pl.ds(j * piece + s * sub, sub), pl.ds(h * HALF, HALF)]

    def scatter(h, j, s):
        k = lax.rem(r, ratio) * C + j
        i = h * nsub + s
        return remote(source_at(h, j, s), prow(h, k, s), sc_s.at[i * C + j], sc_r.at[i], k, r // ratio)

    def is_self(j):
        return jnp.logical_and(r // ratio == 0, lax.rem(r, ratio) * C + j == r)

    def local(h, j, s):
        k = lax.rem(r, ratio) * C + j
        return pltpu.make_async_copy(source_at(h, j, s), prow(h, k, s), lsem.at[h * nsub + s])

    @pl.when(c == 0)
    def _():
        for h in range(2):
            for s in range(nsub):
                for j in range(C):
                    @pl.when(is_self(j))
                    def _():
                        local(h, j, s).start()

                    @pl.when(jnp.logical_not(is_self(j)))
                    def _():
                        scatter(h, j, s).start()

    def gather(h, d, s):
        to = lax.rem(chip + d, chips) * 2 + core
        i = ((d - 1) * 2 + h) * nsub + s
        return remote(prow(h, r, s), prow(h, r, s), pg_s.at[i], pg_r.at[i], to, c)

    def to_sib(h, d, s):
        k = lax.rem(chip + chips - d, chips) * 2 + core
        i = (d * 2 + h) * nsub + s
        return remote(prow(h, k, s), prow(h, k, s), sb_s.at[i], sb_r.at[i], sib, c)

    def relay(h, s):
        @pl.when(self_fed)
        def _():
            local(h, 0, s).wait()

        @pl.when(jnp.logical_not(self_fed))
        def _():
            i = h * nsub + s
            remote(prow(h, r, s), prow(h, r, s), sc_s.at[i], sc_r.at[i], sib, c).wait_recv()

        for d in range(1, chips):
            gather(h, d, s).start()
        to_sib(h, 0, s).start()

    def relay_in(h, s):
        for d in range(1, chips):
            gather(h, d, s).wait_recv()
            to_sib(h, d, s).start()

    def complete(h):
        for s in range(nsub):
            for d in range(chips):
                to_sib(h, d, s).wait_recv()

    def y_copy(t, d):
        to = lax.rem(c + d, C)
        i = t * (C - 1) + d - 1
        return remote(ybuf.at[t, pl.ds(pl.multiple_of(to * q, q), q)], rbuf.at[i], y_s.at[i], y_r.at[i], r, to)

    def first(h, t, carry):
        tt = h * T + t
        slot = lax.rem(tt, 2)
        load_g(tt).wait()
        yacc[...] = jnp.zeros_like(yacc)

        def step(k, carry):
            at = pl.ds(pl.multiple_of(k * TK, TK), TK)
            yacc[...] += jnp.dot(gbuf[slot, :, at], panel[h, at, :], preferred_element_type=jnp.float32)
            return carry

        lax.fori_loop(0, kdim // TK, step, 0)

        @pl.when(tt + 2 < 2 * T)
        def _():
            load_g(tt + 2).start()

        ybuf[tt] = yacc[...].astype(jnp.bfloat16)
        own[tt] = yacc[pl.ds(pl.multiple_of(c * q, q), q), :]
        for d in range(1, C):
            y_copy(tt, d).start()
        return carry

    def ag(t, s, way):
        owner, to = (c - s, c + 1) if way == 0 else (c + s, c - 1)
        i = (t * (C - 1) + s) * 2 + way
        block = image.at[t, pl.ds(pl.multiple_of(owner * q, q), q)]
        return remote(block, block, ag_s.at[i], ag_r.at[i], r, to)

    def ag_cond(s, way):
        if way == 0:
            return jnp.logical_and(c - s >= 0, c + 1 < C)
        return jnp.logical_and(c + s < C, c - 1 >= 0)

    def ag_recv(t, s, way):
        owner = c - s if way == 0 else c + s
        i = (t * (C - 1) + s - 1) * 2 + way
        block = image.at[t, pl.ds(pl.multiple_of(owner * q, q), q)]
        return remote(block, block, ag_s.at[i], ag_r.at[i], r, lax.rem(c + 1, C))

    def send_on(t, s):
        for way in range(2):
            @pl.when(ag_cond(s, way))
            def _():
                ag(t, s, way).start()

    def second(h, u, carry):
        @pl.when(u < T)
        def _():
            tt = h * T + u
            total = own[tt]
            for d in range(1, C):
                y_copy(tt, d).wait_recv()
                total = total + rbuf[tt * (C - 1) + d - 1].astype(jnp.float32)
            image[tt, pl.ds(pl.multiple_of(c * q, q), q)] = total.astype(jnp.bfloat16)
            send_on(tt, 0)

        for s in range(1, C):
            t = u - s

            @pl.when(jnp.logical_and(t >= 0, t < T))
            def _():
                tt = h * T + t

                @pl.when(c - s >= 0)
                def _():
                    ag_recv(tt, s, 0).wait_recv()

                @pl.when(c + s < C)
                def _():
                    ag_recv(tt, s, 1).wait_recv()

                if s < C - 1:
                    send_on(tt, s)

        @pl.when(u >= C - 1)
        def _():
            tt = h * T + u - (C - 1)
            slot = lax.rem(tt, 2)
            load_v(tt).wait()
            image_t[...] = image[tt].T

            def step(n, carry):
                at = pl.ds(pl.multiple_of(n * TN, TN), TN)
                acc[h, :, at] += jnp.dot(image_t[...], vbuf[slot, :, at], preferred_element_type=jnp.float32)
                return carry

            lax.fori_loop(0, width // TN, step, 0)

            @pl.when(tt + 2 < 2 * T)
            def _():
                load_v(tt + 2).start()

        return carry

    def arow(h, k):
        return acc.at[h, pl.ds(pl.multiple_of(k * hp, hp), hp)]

    def pair(h, d):
        to = lax.rem(chip + d, chips)
        i = h * chips + d
        return remote(arow(h, to * 2 + 1 - core), sbuf.at[i], ps_s.at[i], ps_r.at[i], sib, c)

    def spread(h, d):
        k = lax.rem(chip + d, chips) * 2 + core
        i = h * (chips - 1) + d - 1
        return remote(arow(h, k), obuf.at[i], os_s.at[i], os_r.at[i], k, c)

    order = list(range(1, chips)) + [0]

    def out_pair(h):
        for d in order:
            pair(h, d).start()

    def out_spread(h):
        for d in order:
            pair(h, d).wait_recv()
            k = lax.rem(chip + d, chips) * 2 + core
            at = pl.ds(pl.multiple_of(k * hp, hp), hp)
            acc[h, at, :] += sbuf[h * chips + d]
            if d:
                spread(h, d).start()

    def out_sum(h):
        total = acc[h, pl.ds(pl.multiple_of(r * hp, hp), hp), :]
        for d in range(1, chips):
            spread(h, d).wait_recv()
            total = total + obuf[h * (chips - 1) + d - 1]
        out[pl.ds(h * hp, hp), :] = total

    acc[...] = jnp.zeros_like(acc)
    for s in range(nsub):
        relay(0, s)
        if s:
            relay_in(0, s - 1)
    relay_in(0, nsub - 1)
    complete(0)
    for s in range(nsub):
        relay(1, s)
        lax.fori_loop(T * s // nsub, T * (s + 1) // nsub, functools.partial(first, 0), 0)
        if s:
            relay_in(1, s - 1)
    relay_in(1, nsub - 1)
    complete(1)
    steps = T + C - 1

    def both(t, carry):
        return second(0, t, first(1, t, carry))

    lax.fori_loop(0, T, both, 0)
    lax.fori_loop(T, steps, functools.partial(second, 0), 0)
    out_pair(0)
    lax.fori_loop(0, 1, functools.partial(second, 1), 0)
    out_spread(0)
    lax.fori_loop(1, steps, functools.partial(second, 1), 0)
    out_pair(1)
    out_sum(0)
    out_spread(1)
    out_sum(1)

    for h in range(2):
        @pl.when(c == 0)
        def _():
            for s in range(nsub):
                for j in range(C):
                    @pl.when(jnp.logical_not(is_self(j)))
                    def _():
                        scatter(h, j, s).wait_send()

        for s in range(nsub):
            for d in range(1, chips):
                gather(h, d, s).wait_send()
            for d in range(chips):
                to_sib(h, d, s).wait_send()

    def drain(t, carry):
        for d in range(1, C):
            y_copy(t, d).wait_send()
        for s in range(C - 1):
            for way in range(2):
                @pl.when(ag_cond(s, way))
                def _():
                    ag(t, s, way).wait_send()
        return carry

    lax.fori_loop(0, 2 * T, drain, 0)
    for h in range(2):
        for d in range(chips):
            pair(h, d).wait_send()
        for d in range(1, chips):
            spread(h, d).wait_send()


def shards(R, C, gradient, sensitivity):
    rows, kdim = gradient.shape
    width = sensitivity.shape[1]
    TM = 512 if rows % 512 == 0 else 256
    T, q, piece, po, chips = rows // TM, TM // C, kdim // R, PANEL // R, R // 2
    hp = po // 2
    nsub = 4 if piece % 64 == 0 else 1
    n = jnp.arange(PANEL)
    h, k, i = n // HALF, n % HALF // hp, n % hp
    taken = k * po + h * hp + i
    pick = (jnp.arange(PANEL)[:, None] == taken[None, :]).astype(jnp.bfloat16)
    source = jnp.dot(sensitivity[:, :PANEL], pick, preferred_element_type=jnp.bfloat16)
    dma = lambda n: pltpu.SemaphoreType.DMA((n,))
    return pl.pallas_call(
        functools.partial(kernel, R, C, TM),
        out_shape=jax.ShapeDtypeStruct((po, width), jnp.float32),
        in_specs=[pl.BlockSpec(memory_space=pl.ANY)] * 3,
        out_specs=pl.BlockSpec(memory_space=pltpu.VMEM),
        scratch_shapes=[
            pltpu.VMEM((2, kdim, HALF), jnp.bfloat16),
            pltpu.VMEM((2 * T, TM, HALF), jnp.bfloat16),
            pltpu.VMEM((2 * T, q, HALF), jnp.float32),
            pltpu.VMEM((2 * T * (C - 1), q, HALF), jnp.bfloat16),
            pltpu.VMEM((2 * T, TM, HALF), jnp.bfloat16),
            pltpu.VMEM((2, HALF, width), jnp.float32),
            pltpu.VMEM((2 * chips, hp, width), jnp.float32),
            pltpu.VMEM((2 * (chips - 1), hp, width), jnp.float32),
            pltpu.VMEM((2, TM, kdim), jnp.bfloat16),
            pltpu.VMEM((2, TM, width), jnp.bfloat16),
            pltpu.VMEM((TM, HALF), jnp.float32),
            pltpu.VMEM((HALF, TM), jnp.bfloat16),
            dma(2), dma(2), dma(2 * nsub),
            dma(2 * C * nsub), dma(2 * nsub),
            dma(2 * (chips - 1) * nsub), dma(2 * (chips - 1) * nsub),
            dma(2 * chips * nsub), dma(2 * chips * nsub),
            dma(2 * T * (C - 1)), dma(2 * T * (C - 1)),
            dma(4 * T * (C - 1)), dma(4 * T * (C - 1)),
            dma(2 * chips), dma(2 * chips),
            dma(2 * (chips - 1)), dma(2 * (chips - 1)),
        ],
        compiler_params=pltpu.CompilerParams(
            collective_id=0, has_side_effects=True, vmem_limit_bytes=60 * 2**20
        ),
    )(gradient, sensitivity, source)


def solution(mesh):
    R, C = mesh.shape["row"], mesh.shape["col"]
    return jax.shard_map(
        functools.partial(shards, R, C),
        mesh=mesh,
        in_specs=(P("row", "col"), P("row", "col")),
        out_specs=P("row", "col"),
        check_vma=False,
    )
```
